32 devices in a mesh: ctx: 8 (over z, core), tp: 4 (over y, x).
Axes of the slice: x: 2, y: 2, z: 4, core: 2. Of those that a mesh axis runs over, the one named last changes fastest.
Arguments:
- queries: bfloat16 [4096, 4096], P('ctx', 'tp'), may hold values from -140 to 140
- key_vecs: bfloat16 [4096, 1024], P('ctx', 'tp'), may hold values from -6 to 6
- value_vecs: bfloat16 [4096, 1024], P('ctx', 'tp'), may hold values from -6 to 6
- out_grad: bfloat16 [4096, 4096], P('ctx', 'tp'), may hold values from -6 to 6
- doc_ids: int32 [32], replicated, may hold values from 0 to 9, never falling along the last dimension, each value on 1 to 8 neighbouring positions
Outputs:
- attended: bfloat16 [4096, 4096], P('ctx', 'tp')
- query_grad: bfloat16 [4096, 4096], P('ctx', 'tp')
- key_grad: bfloat16 [4096, 1024], P('ctx', 'tp')
- value_grad: bfloat16 [4096, 1024], P('ctx', 'tp')
The draws below stay inside these ranges and needn't reach their ends.
Inputs may be any that keep to these rules, and one draw needn't show every extreme that they name: doc_ids never fall along the sequence; each document covers 1 to 8 blocks and one covers exactly 8.
All inputs are finite; a program needn't handle non-finite values.
Results may differ from the reference program's by a relative error of at most 0.0075.
Values may be sent and summed in bfloat16 or wider, within the bound.
No kernel may reach another device: no remote copies, remote signals or barrier semaphores. Data moves between devices by JAX's collectives and lax.ppermute only.
A program may use at most 64 MiB of HBM per device.

```python
import math
import jax
import jax.numpy as jnp
import numpy as np
from jax import lax

QH = 32
KVH = 8
HD = 128
BLK = 128
REACH = 2
TOK_DEV = 512
TOKENS = 4096
NBLK = 32
MOST_BLK = 8
DOCS = 10
N_CTX = 8


def joint_draw(key):
    noise_query = jnp.clip(jax.random.normal(jax.random.fold_in(key, 11), (TOKENS, QH * HD), jnp.float32), -6.0, 6.0)
    noise_key = jnp.clip(jax.random.normal(jax.random.fold_in(key, 12), (TOKENS, KVH * HD), jnp.float32), -6.0, 6.0)
    return (noise_query, noise_key)


def draw_queries(key, part):
    return joint_draw(key)[0].astype(jnp.bfloat16)


def draw_key_vecs(key, part):
    return joint_draw(key)[1].astype(jnp.bfloat16)


def draw_out_grad(key, part):
    noise_grad = jnp.clip(jax.random.normal(jax.random.fold_in(key, 21), (TOKENS, QH * HD), jnp.float32), -6.0, 6.0)
    return noise_grad.astype(jnp.bfloat16)


def levels(stream_key, dims, split, low, high):
    def one(axis_at, shards_of):
        heights = jax.random.uniform(jax.random.fold_in(jax.random.fold_in(stream_key, 6), axis_at), (shards_of,), jnp.float32, low / len(split), high / len(split))
        return jnp.repeat(jnp.exp(heights), dims[axis_at] // shards_of).reshape((-1,) + (1,) * (len(dims) - axis_at - 1))

    gain = one(*split[0])
    for cut in split[1:]:
        gain = gain * one(*cut)
    return gain


def split_up(number_of, total, limit, lean):
    portions = [(1 << 20) // math.isqrt(rank ** lean) + 1 for rank in range(2, number_of + 1)]
    rest, holding = total - limit - (number_of - 1), [1] * (number_of - 1)
    while rest > 0:
        candidates = [i for i in range(number_of - 1) if holding[i] < limit]
        mass, budget = sum([portions[i] for i in candidates]), rest
        for i in candidates:
            more = min(limit - holding[i], max(1, budget * portions[i] // mass), rest)
            holding[i] = holding[i] + more
            rest = rest - more
    return np.array([limit] + holding)


def ragged(key, number_of, total, reach, slope):
    if number_of == 2:
        one = jax.random.randint(key, (), max(1, total - reach), min(reach, total - 1) + 1)
        return jnp.stack([one, total - one])
    tallies = jnp.asarray(split_up(number_of, total, reach, slope), jnp.int32)
    pairs = (number_of - 1) // 2
    giver, sink = tallies[1:1 + 2 * pairs:2], tallies[2:2 + 2 * pairs:2]
    room = jnp.minimum(giver - 1, reach - sink)
    moved = jax.random.randint(jax.random.fold_in(key, 1), (pairs,), 0, 1 << 20) % (room + 1)
    tallies = tallies.at[1:1 + 2 * pairs:2].set(giver - moved).at[2:2 + 2 * pairs:2].set(sink + moved)
    return tallies[jax.random.permutation(jax.random.fold_in(key, 2), number_of)]


def bell_draw(own_key, dims, width, limit, split=(), kind=jnp.bfloat16):
    array = jax.random.normal(own_key, dims, jnp.float32) * width
    if len(split) > 0:
        array = levels(own_key, dims, split, -0.22, 0.18) * array
    return jnp.clip(array, min=-limit, max=limit).astype(kind)


def setup_inputs(seed: int = 0) -> dict:
    streams_of = jax.random.split(jax.random.key(seed), 6)
    return {
        "queries": draw_queries(jax.random.fold_in(streams_of[5], 71), 0),
        "key_vecs": draw_key_vecs(jax.random.fold_in(streams_of[5], 71), 0),
        "value_vecs": bell_draw(streams_of[2], (TOKENS, KVH * HD), 1.0, 6.0, ((0, 8), (1, 4))),
        "out_grad": draw_out_grad(jax.random.fold_in(streams_of[5], 71), 0),
        "doc_ids": jnp.searchsorted(jnp.cumsum(ragged(streams_of[4], DOCS, NBLK, MOST_BLK, 2)), jnp.arange(NBLK), side="right").astype(jnp.int32),
    }


negative_fill = -1.0e30


def reference(queries, key_vecs, value_vecs, out_grad, doc_ids):
    length_dev = TOK_DEV
    window = (REACH + 1) * length_dev
    lead = REACH * length_dev
    group_size = QH // KVH
    scale_factor = HD ** -0.5
    blocks_dev = length_dev // BLK
    zero_rows = jnp.zeros((lead, KVH * HD), jnp.bfloat16)
    keys_pad = jnp.concatenate([zero_rows, key_vecs], axis=0)
    values_pad = jnp.concatenate([zero_rows, value_vecs], axis=0)
    docs_pad = jnp.concatenate([jnp.full((REACH * blocks_dev,), -1, jnp.int32), doc_ids.astype(jnp.int32)])

    def step(carry, index):
        key_acc, value_acc = carry
        start = (index * length_dev).astype(jnp.int32)
        query_part = lax.dynamic_slice_in_dim(queries, start, length_dev, 0).astype(jnp.float32).reshape(length_dev, KVH, group_size, HD)
        grad_part = lax.dynamic_slice_in_dim(out_grad, start, length_dev, 0).astype(jnp.float32).reshape(length_dev, KVH, group_size, HD)
        key_part = lax.dynamic_slice_in_dim(keys_pad, start, window, 0).astype(jnp.float32).reshape(window, KVH, HD)
        value_part = lax.dynamic_slice_in_dim(values_pad, start, window, 0).astype(jnp.float32).reshape(window, KVH, HD)
        block_start = (index * blocks_dev).astype(jnp.int32)
        query_docs = jnp.repeat(lax.dynamic_slice_in_dim(doc_ids.astype(jnp.int32), block_start, blocks_dev, 0), BLK)
        key_docs = jnp.repeat(lax.dynamic_slice_in_dim(docs_pad, block_start, window // BLK, 0), BLK)
        query_pos = start + jnp.arange(length_dev, dtype=jnp.int32)
        key_pos = start - lead + jnp.arange(window, dtype=jnp.int32)
        allowed = (query_docs[:, None] == key_docs[None, :]) & (key_pos[None, :] <= query_pos[:, None]) & (key_pos[None, :] >= 0)
        scores = jnp.einsum("qhgd,khd->hgqk", query_part, key_part) * scale_factor
        highest = jnp.max(jnp.where(allowed, scores, negative_fill), axis=-1, keepdims=True)
        total = jnp.sum(jnp.where(allowed, jnp.exp(scores - highest), 0.0), axis=-1, keepdims=True)
        lse = highest + jnp.log(total)
        probs = jnp.where(allowed, jnp.exp(scores - lse), 0.0)
        probs16 = probs.astype(jnp.bfloat16)
        output = jnp.einsum("hgqk,khd->qhgd", probs16.astype(jnp.float32), value_part)
        output16 = output.astype(jnp.bfloat16)
        delta = jnp.sum(grad_part * output16.astype(jnp.float32), axis=-1)
        delta_hgq = jnp.transpose(delta, (1, 2, 0))
        dprobs = jnp.einsum("qhgd,khd->hgqk", grad_part, value_part)
        dscores = (probs * (dprobs - delta_hgq[..., None])).astype(jnp.bfloat16).astype(jnp.float32)
        query_grad = jnp.einsum("hgqk,khd->qhgd", dscores, key_part) * scale_factor
        key_term = jnp.einsum("hgqk,qhgd->khd", dscores, query_part) * scale_factor
        value_term = jnp.einsum("hgqk,qhgd->khd", probs16.astype(jnp.float32), grad_part)
        key_acc = lax.dynamic_update_slice_in_dim(key_acc, lax.dynamic_slice_in_dim(key_acc, start, window, 0) + key_term.reshape(window, KVH * HD), start, 0)
        value_acc = lax.dynamic_update_slice_in_dim(value_acc, lax.dynamic_slice_in_dim(value_acc, start, window, 0) + value_term.reshape(window, KVH * HD), start, 0)
        return (key_acc, value_acc), (output16.reshape(length_dev, QH * HD), query_grad.astype(jnp.bfloat16).reshape(length_dev, QH * HD))

    start_acc = jnp.zeros((lead + TOKENS, KVH * HD), jnp.float32)
    (key_acc, value_acc), (outputs, query_grads) = lax.scan(step, (start_acc, start_acc), jnp.arange(N_CTX, dtype=jnp.int32))
    attended = outputs.reshape(TOKENS, QH * HD)
    query_grad = query_grads.reshape(TOKENS, QH * HD)
    key_grad = key_acc[lead:].astype(jnp.bfloat16)
    value_grad = value_acc[lead:].astype(jnp.bfloat16)
    return (attended, query_grad, key_grad, value_grad)
```

```python
import functools

import jax
import jax.numpy as jnp
from jax import lax
from jax.experimental import pallas as pl
from jax.experimental.pallas import tpu as pltpu
from jax.sharding import PartitionSpec as P

QH = 32
KVH = 8
HD = 128
BLK = 128
MOST_BLK = 8
GROUP = QH // KVH
SCALE = HD ** (-0.5)
LOG2E = 1.4426950408889634
SCALE2 = SCALE * LOG2E
negative_fill = -1e30
F32 = jnp.float32
BF16 = jnp.bfloat16


def turn(block, step):
    n = lax.axis_size("ctx")
    return lax.ppermute(block, "ctx", [(i, (i + step) % n) for i in range(n)])


def dot(a, b):
    return lax.dot_general(a, b, (((1,), (0,)), ((), ())), preferred_element_type=F32)


def dot_nt(a, b):
    return lax.dot_general(a, b, (((1,), (1,)), ((), ())), preferred_element_type=F32)


def stack_heads(x):
    return jnp.concatenate([x[:, g * HD : (g + 1) * HD] for g in range(GROUP)], axis=0)


def spread_heads(x):
    rows = x.shape[0] // GROUP
    return jnp.concatenate([x[g * rows : (g + 1) * rows] for g in range(GROUP)], axis=1)


def blocks_behind(docs_ref, index):
    doc = docs_ref[index]
    count = jnp.int32(0)
    for d in range(1, MOST_BLK):
        same = (index >= d) & (docs_ref[jnp.maximum(index - d, 0)] == doc)
        count = count + jnp.where(same, 1, 0)
    return count


def biased(s, first, start):
    parts = []
    for b in range(s.shape[0] // BLK):
        bias = jnp.where(first + b >= start, 0.0, negative_fill).astype(F32)
        parts.append(s[b * BLK : (b + 1) * BLK] * SCALE2 + bias)
    return parts


def causal(part):
    key = lax.broadcasted_iota(jnp.int32, part.shape, 0)
    query = lax.broadcasted_iota(jnp.int32, part.shape, 1) % BLK
    return jnp.where(key <= query, part, negative_fill)


def own_scores(k, qs, i, behind):
    parts = biased(dot_nt(k[: (i + 1) * BLK], qs), 0, i - behind)
    parts[i] = causal(parts[i])
    return jnp.concatenate(parts, axis=0)


def own_forward(blocks_dev, docs_ref, q_ref, k_ref, v_ref, stats_ref, o_ref):
    base = lax.axis_index("ctx") * blocks_dev
    k = k_ref[...]
    v_t = v_ref[...].T
    for i in range(blocks_dev):
        qs = stack_heads(q_ref[i * BLK : (i + 1) * BLK, :])
        s = own_scores(k, qs, i, blocks_behind(docs_ref, base + i))
        m = jnp.max(s, axis=0, keepdims=True)
        p = jnp.exp2(s - m)
        stats_ref[0, i : i + 1, :] = m
        stats_ref[0, blocks_dev + i : blocks_dev + i + 1, :] = jnp.sum(p, axis=0, keepdims=True)
        o_ref[0, i] = dot(v_t[:, : (i + 1) * BLK], p.astype(BF16))


def far_part(blocks_dev, aliased, docs_ref, q_ref, g_ref, kv1_ref, kv2_ref, stats_ref, o0_ref, *rest):
    rest = rest[1:] if aliased else rest
    att_ref, dq_ref, ls_ref, d1_ref, d2_ref, acc_k, acc_v = rest
    i = pl.program_id(0)
    near = blocks_dev * BLK
    far = kv2_ref.shape[0]
    reach = (near + far) // BLK
    behind = blocks_behind(docs_ref, lax.axis_index("ctx") * blocks_dev + i)
    start = reach + i - behind

    @pl.when(i == 0)
    def _():
        acc_k[...] = jnp.zeros_like(acc_k)
        acc_v[...] = jnp.zeros_like(acc_v)

    m0 = stats_ref[0, pl.ds(i, 1), :]
    l0 = stats_ref[0, pl.ds(blocks_dev + i, 1), :]

    def give(o_t, m, l):
        o16 = o_t.astype(BF16).T
        att_ref[...] = spread_heads(o16)
        x = o16.astype(F32) * stack_heads(g_ref[...]).astype(F32)
        high = x.astype(BF16)
        low = (x - high.astype(F32)).astype(BF16)
        ones = jnp.ones((8, HD), BF16)
        delta = (dot_nt(ones, high) + dot_nt(ones, low))[:1]
        ls_ref[0, pl.ds(i, 1), :] = m + jnp.log2(l)
        ls_ref[0, pl.ds(blocks_dev + i, 1), :] = delta
        return delta

    def work(lo):
        def cols(c):
            piece = kv1_ref[:, c * HD : (c + 1) * HD]
            if lo < far:
                piece = jnp.concatenate([kv2_ref[lo:, c * HD : (c + 1) * HD], piece], axis=0)
            return piece

        qs = stack_heads(q_ref[...])
        gs = stack_heads(g_ref[...])
        k, v = cols(0), cols(1)
        s = jnp.concatenate(biased(dot_nt(k, qs), lo // BLK, start), axis=0)
        m = jnp.maximum(m0, jnp.max(s, axis=0, keepdims=True))
        p = jnp.exp2(s - m)
        shrink = jnp.exp2(m0 - m)
        l = l0 * shrink + jnp.sum(p, axis=0, keepdims=True)
        inv = 1.0 / l
        p = p * inv
        p16 = p.astype(BF16)
        acc_v[lo:, :] += dot(p16, gs)
        delta = give(dot(v.T, p16) + o0_ref[0, 0] * (shrink * inv), m, l)
        ds = (p * (dot_nt(v, gs) - delta)).astype(BF16)
        acc_k[lo:, :] += dot(ds, qs)
        dq_ref[0] = dot(k.T, ds)

    @pl.when(start >= reach)
    def _():
        give(o0_ref[0, 0] * (1.0 / l0), m0, l0)
        dq_ref[0] = jnp.zeros_like(dq_ref[0])

    @pl.when((start < reach) & (start >= far // BLK))
    def _():
        work(far)

    @pl.when(start < far // BLK)
    def _():
        work(0)

    @pl.when(i == pl.num_programs(0) - 1)
    def _():
        d2_ref[:, :HD] = (acc_k[:far] * SCALE).astype(BF16)
        d2_ref[:, HD:] = acc_v[:far].astype(BF16)
        d1_ref[:, :HD] = (acc_k[far:] * SCALE).astype(BF16)
        d1_ref[:, HD:] = acc_v[far:].astype(BF16)


def own_backward(blocks_dev, aliased, docs_ref, q_ref, g_ref, k_ref, v_ref, ls_ref, dqf_ref, *rest):
    query_ref, dk_ref, dv_ref = rest[1:] if aliased else rest
    base = lax.axis_index("ctx") * blocks_dev
    k = k_ref[...]
    v = v_ref[...]
    k_t = k.T
    dk_ref[...] = jnp.zeros_like(dk_ref)
    dv_ref[...] = jnp.zeros_like(dv_ref)

    for i in range(blocks_dev):
        n = (i + 1) * BLK
        qs = stack_heads(q_ref[i * BLK : n, :])
        gs = stack_heads(g_ref[i * BLK : n, :])
        s = own_scores(k, qs, i, blocks_behind(docs_ref, base + i))
        p = jnp.exp2(s - ls_ref[0, i : i + 1, :])
        dv_ref[:n, :] += dot(p.astype(BF16), gs)
        delta = ls_ref[0, blocks_dev + i : blocks_dev + i + 1, :]
        ds = (p * (dot_nt(v[:n], gs) - delta)).astype(BF16)
        dk_ref[:n, :] += dot(ds, qs)
        dq = (dot(k_t[:, :n], ds) + dqf_ref[i]) * SCALE
        query_ref[i * BLK : n, :] = spread_heads(dq.astype(BF16).T)
    dk_ref[...] *= SCALE


def body(queries, key_vecs, value_vecs, out_grad, doc_ids):
    length_dev = queries.shape[0]
    blocks_dev = length_dev // BLK
    heads = key_vecs.shape[1] // HD
    lanes = GROUP * BLK
    far = (MOST_BLK - 1 - blocks_dev) * BLK
    wide = GROUP * HD
    params = pltpu.CompilerParams(vmem_limit_bytes=32 << 20)
    smem = pl.BlockSpec(memory_space=pltpu.SMEM)
    shape = jax.ShapeDtypeStruct

    def col(h):
        return slice(h * HD, (h + 1) * HD)

    pairs = [jnp.concatenate([key_vecs[:, col(h)], value_vecs[:, col(h)]], axis=1) for h in range(heads)]
    kv1 = [turn(pair, 1) for pair in pairs]

    stats, o0 = pl.pallas_call(
        functools.partial(own_forward, blocks_dev),
        name="own_forward",
        grid=(heads,),
        in_specs=[
            smem,
            pl.BlockSpec((length_dev, wide), lambda h: (0, h)),
            pl.BlockSpec((length_dev, HD), lambda h: (0, h)),
            pl.BlockSpec((length_dev, HD), lambda h: (0, h)),
        ],
        out_specs=[
            pl.BlockSpec((1, 2 * blocks_dev, lanes), lambda h: (h, 0, 0)),
            pl.BlockSpec((1, blocks_dev, HD, lanes), lambda h: (h, 0, 0, 0)),
        ],
        out_shape=[
            shape((heads, 2 * blocks_dev, lanes), F32),
            shape((heads, blocks_dev, HD, lanes), F32),
        ],
        compiler_params=params,
    )(doc_ids, queries, key_vecs, value_vecs)

    kv2 = [turn(kv[length_dev - far :], 1) for kv in kv1]

    attended = None
    stats_out, dq_far, near_back, far_back = [], [], [], []
    for h in range(heads):
        aliased = attended is not None
        at = lambda i, h=h: (i, h)
        in_specs = [
            smem,
            pl.BlockSpec((BLK, wide), at),
            pl.BlockSpec((BLK, wide), at),
            pl.BlockSpec((length_dev, 2 * HD), lambda i: (0, 0)),
            pl.BlockSpec((far, 2 * HD), lambda i: (0, 0)),
            pl.BlockSpec((1, 2 * blocks_dev, lanes), lambda i, h=h: (h, 0, 0)),
            pl.BlockSpec((1, 1, HD, lanes), lambda i, h=h: (h, i, 0, 0)),
        ]
        args = [doc_ids, queries, out_grad, kv1[h], kv2[h], stats, o0]
        if aliased:
            in_specs.append(pl.BlockSpec(memory_space=pl.ANY))
            args.append(attended)
        attended, dq, ls, d1, d2 = pl.pallas_call(
            functools.partial(far_part, blocks_dev, aliased),
            name="far_part",
            grid=(blocks_dev,),
            in_specs=in_specs,
            out_specs=[
                pl.BlockSpec((BLK, wide), at),
                pl.BlockSpec((1, HD, lanes), lambda i: (i, 0, 0)),
                pl.BlockSpec((1, 2 * blocks_dev, lanes), lambda i: (0, 0, 0)),
                pl.BlockSpec((length_dev, 2 * HD), lambda i: (0, 0)),
                pl.BlockSpec((far, 2 * HD), lambda i: (0, 0)),
            ],
            out_shape=[
                shape(queries.shape, BF16),
                shape((blocks_dev, HD, lanes), F32),
                shape((1, 2 * blocks_dev, lanes), F32),
                shape((length_dev, 2 * HD), BF16),
                shape((far, 2 * HD), BF16),
            ],
            scratch_shapes=[pltpu.VMEM((length_dev + far, HD), F32)] * 2,
            input_output_aliases={len(args) - 1: 0} if aliased else {},
            compiler_params=params,
        )(*args)
        stats_out.append(ls)
        dq_far.append(dq)
        near_back.append(d1)
        far_back.append(turn(d2, -1))

    whole_back = []
    for h in range(heads):
        joined = near_back[h].astype(F32) + jnp.pad(far_back[h].astype(F32), ((length_dev - far, 0), (0, 0)))
        whole_back.append(turn(joined.astype(BF16), -1))

    query_grad = None
    own = []
    for h in range(heads):
        aliased = query_grad is not None
        in_specs = [
            smem,
            pl.BlockSpec((length_dev, wide), lambda z, h=h: (0, h)),
            pl.BlockSpec((length_dev, wide), lambda z, h=h: (0, h)),
            pl.BlockSpec((length_dev, HD), lambda z, h=h: (0, h)),
            pl.BlockSpec((length_dev, HD), lambda z, h=h: (0, h)),
            pl.BlockSpec((1, 2 * blocks_dev, lanes), lambda z: (0, 0, 0)),
            pl.BlockSpec((blocks_dev, HD, lanes), lambda z: (0, 0, 0)),
        ]
        args = [doc_ids, queries, out_grad, key_vecs, value_vecs, stats_out[h], dq_far[h]]
        if aliased:
            in_specs.append(pl.BlockSpec(memory_space=pl.ANY))
            args.append(query_grad)

        query_grad, dk, dv = pl.pallas_call(
            functools.partial(own_backward, blocks_dev, aliased),
            name="own_backward",
            grid=(1,),
            in_specs=in_specs,
            out_specs=[
                pl.BlockSpec((length_dev, wide), lambda z, h=h: (0, h)),
                pl.BlockSpec((length_dev, HD), lambda z: (0, 0)),
                pl.BlockSpec((length_dev, HD), lambda z: (0, 0)),
            ],
            out_shape=[
                shape(queries.shape, BF16),
                shape((length_dev, HD), F32),
                shape((length_dev, HD), F32),
            ],
            input_output_aliases={len(args) - 1: 0} if aliased else {},
            compiler_params=params,
        )(*args)
        own.append((dk, dv))

    def finish(*refs):
        dk_out, dv_out = refs[3 * heads :]
        for h in range(heads):
            dk_ref, dv_ref, back_ref = refs[3 * h : 3 * h + 3]
            dk_out[:, col(h)] = (dk_ref[...] + back_ref[:, :HD].astype(F32)).astype(BF16)
            dv_out[:, col(h)] = (dv_ref[...] + back_ref[:, HD:].astype(F32)).astype(BF16)

    args = [x for h in range(heads) for x in (*own[h], whole_back[h])]
    key_grad, value_grad = pl.pallas_call(
        finish,
        name="finish",
        out_shape=[shape(key_vecs.shape, BF16)] * 2,
        compiler_params=params,
    )(*args)
    return (attended, query_grad, key_grad, value_grad)


def solution(mesh):
    placed = (P("ctx", "tp"), P("ctx", "tp"), P("ctx", "tp"), P("ctx", "tp"), P())
    return jax.shard_map(
        body,
        mesh=mesh,
        in_specs=placed,
        out_specs=(P("ctx", "tp"), P("ctx", "tp"), P("ctx", "tp"), P("ctx", "tp")),
        check_vma=False,
    )
```

```python
import functools

import jax
import jax.numpy as jnp
from jax import lax
from jax.experimental import pallas as pl
from jax.experimental.pallas import tpu as pltpu
from jax.sharding import PartitionSpec as P

QH = 32
KVH = 8
HD = 128
BLK = 128
MOST_BLK = 8
GROUP = QH // KVH
SCALE = HD ** (-0.5)
WIDE = GROUP * HD
LOG2E = 1.4426950408889634
SCALE2 = SCALE * LOG2E
negative_fill = -1e30
F32 = jnp.float32
BF16 = jnp.bfloat16


def turn(block, step):
    n = lax.axis_size("ctx")
    return lax.ppermute(block, "ctx", [(i, (i + step) % n) for i in range(n)])


def dot(a, b):
    return lax.dot_general(a, b, (((1,), (0,)), ((), ())), preferred_element_type=F32)


def dot_nt(a, b):
    return lax.dot_general(a, b, (((1,), (1,)), ((), ())), preferred_element_type=F32)


def stack_heads(x):
    return jnp.concatenate([x[:, g * HD : (g + 1) * HD] for g in range(GROUP)], axis=0).T


def spread_heads(x):
    x = x.T
    rows = x.shape[0] // GROUP
    return jnp.concatenate([x[g * rows : (g + 1) * rows] for g in range(GROUP)], axis=1)


def blocks_behind(docs_ref, index):
    doc = docs_ref[index]
    count = jnp.int32(0)
    for d in range(1, MOST_BLK):
        same = (index >= d) & (docs_ref[jnp.maximum(index - d, 0)] == doc)
        count = count + jnp.where(same, 1, 0)
    return count


def crossing(docs_ref, base, blocks_dev):
    behind = blocks_behind(docs_ref, base)
    here = jnp.int32(0)
    for i in range(blocks_dev):
        here = here + jnp.where(docs_ref[base + i] == docs_ref[base], 1, 0)
    return behind, jnp.where(behind > 0, here, 0)


def biased(s, first, start):
    parts = []
    for b in range(s.shape[0] // BLK):
        bias = jnp.where(first + b >= start, 0.0, negative_fill).astype(F32)
        parts.append(s[b * BLK : (b + 1) * BLK] * SCALE2 + bias)
    return parts


def causal(part):
    key = lax.broadcasted_iota(jnp.int32, part.shape, 0)
    query = lax.broadcasted_iota(jnp.int32, part.shape, 1) % BLK
    return jnp.where(key <= query, part, negative_fill)


def own_scores(k, q_t, i, behind):
    parts = biased(dot(k[: (i + 1) * BLK], q_t), 0, i - behind)
    parts[i] = causal(parts[i])
    return jnp.concatenate(parts, axis=0)


def delta_of(o16, g_t):
    return jnp.sum(o16.astype(F32) * g_t.astype(F32), axis=0, keepdims=True)


class Store:
    def __init__(self, blocks, sem, whole, head):
        self.blocks, self.sem, self.whole, self.head = blocks, sem, whole, head

    def copy(self, i):
        place = self.whole.at[pl.ds(i * BLK, BLK), pl.ds(self.head * WIDE, WIDE)]
        return pltpu.make_async_copy(self.blocks.at[i], place, self.sem.at[i])

    def put(self, i, x):
        self.blocks[i] = x
        self.copy(i).start()


def own_part(blocks_dev, head, docs_ref, q_ref, g_ref, k_ref, v_ref, att_ref, qt_ref, gt_ref, stats_ref, o_ref, out_ref, sem):
    attended = Store(out_ref, sem, att_ref, head)
    base = lax.axis_index("ctx") * blocks_dev
    wide, slim = slice(head * WIDE, (head + 1) * WIDE), slice(head * HD, (head + 1) * HD)
    k = k_ref[:, slim]
    v_t = v_ref[:, slim].T
    for i in range(blocks_dev):
        rows = slice(i * BLK, (i + 1) * BLK)
        q_t = stack_heads(q_ref[rows, wide])
        g_t = stack_heads(g_ref[rows, wide])
        qt_ref[i] = q_t
        gt_ref[i] = g_t
        s = own_scores(k, q_t, i, blocks_behind(docs_ref, base + i))
        m = jnp.max(s, axis=0, keepdims=True)
        p = jnp.exp2(s - m)
        l = jnp.sum(p, axis=0, keepdims=True)
        o = dot(v_t[:, : (i + 1) * BLK], p.astype(BF16))
        o_ref[i] = o
        o16 = (o * (1.0 / l)).astype(BF16)
        attended.put(i, spread_heads(o16))
        for r, row in enumerate((m, l, m + jnp.log2(l), delta_of(o16, g_t))):
            stats_ref[r * blocks_dev + i : r * blocks_dev + i + 1, :] = row
    for i in range(blocks_dev):
        attended.copy(i).wait()


def own_first(blocks_dev, heads, *refs):
    sources, att_ref, targets, outs = refs[:5], refs[5], refs[6:11], refs[11:15]
    out_ref, sem, docs_smem, read_sem = refs[15:]
    docs = pltpu.make_async_copy(sources[0], docs_smem, read_sem.at[0, 0])
    docs_out = pltpu.make_async_copy(sources[0], targets[0], read_sem.at[0, 1])
    reads = []
    for a in range(1, 5):
        width = sources[a].shape[1] // heads
        for h in range(heads):
            part = (slice(None), pl.ds(h * width, width))
            reads.append((h, pltpu.make_async_copy(sources[a].at[part], targets[a].at[part], read_sem.at[a, h])))
    reads.sort(key=lambda read: read[0])
    docs.start()
    for _, read in reads:
        read.start()
    docs_out.start()
    docs.wait()
    for h, read in reads:
        if h == 0:
            read.wait()
    own_part(blocks_dev, 0, docs_smem, *targets[1:], att_ref, *outs, out_ref, sem)
    for h, read in reads:
        if h > 0:
            read.wait()
    docs_out.wait()


def own_later(blocks_dev, head, docs_ref, q_ref, g_ref, k_ref, v_ref, _, *rest):
    own_part(blocks_dev, head, docs_ref, q_ref, g_ref, k_ref, v_ref, *rest)


def far_part(blocks_dev, head, docs_ref, qt_ref, gt_ref, k1_ref, v1_ref, k2_ref, v2_ref, stats_ref, o0_ref, _, *rest):
    att_ref, dq_ref, ls_ref, d1_ref, d2_ref, acc_k, acc_v, out_ref, sem = rest
    far = k2_ref.shape[0] // BLK
    reach = blocks_dev + far
    behind, here = crossing(docs_ref, lax.axis_index("ctx") * blocks_dev, blocks_dev)
    start = reach - behind
    head_cols = slice(head * HD, (head + 1) * HD)
    attended = Store(out_ref, sem, att_ref, head)
    ls_ref[...] = stats_ref[2 * blocks_dev :, :]
    d1_ref[...] = jnp.zeros_like(d1_ref)
    d2_ref[...] = jnp.zeros_like(d2_ref)

    def pair(lo, first, most):
        def keys(near_ref, far_ref):
            piece = near_ref[:, head_cols]
            if lo < far:
                piece = jnp.concatenate([far_ref[lo * BLK :, head_cols], piece], axis=0)
            return piece

        k, v = keys(k1_ref, k2_ref), keys(v1_ref, v2_ref)
        k_t, v_t = k.T, v.T
        blocks = range(first, min(first + 2, most))
        q_t = [qt_ref[i] for i in blocks]
        g_t = [gt_ref[i] for i in blocks]
        scores = [dot(k, q) for q in q_t]
        ps, p16s, outs, dps = [], [], [], []
        for j, i in enumerate(blocks):
            row = lambda r, i=i: stats_ref[r * blocks_dev + i : r * blocks_dev + i + 1, :]
            first_key = jnp.where(i < here, start, reach)
            s = jnp.concatenate(biased(scores[j], lo, first_key), axis=0)
            m = jnp.maximum(row(0), jnp.max(s, axis=0, keepdims=True))
            p = jnp.exp2(s - m)
            shrink = jnp.exp2(row(0) - m)
            l = row(1) * shrink + jnp.sum(p, axis=0, keepdims=True)
            inv = 1.0 / l
            p = p * inv
            ps.append(p)
            p16s.append(p.astype(BF16))
            ls_ref[i : i + 1, :] = m + jnp.log2(l)
            outs.append(dot(v_t, p16s[j]) + o0_ref[i] * (shrink * inv))
            dps.append(dot(v, g_t[j]))
        dss = []
        for j, i in enumerate(blocks):
            o16 = outs[j].astype(BF16)
            delta = delta_of(o16, g_t[j])
            ls_ref[blocks_dev + i : blocks_dev + i + 1, :] = delta
            dss.append((ps[j] * (dps[j] - delta)).astype(BF16))
            dq_ref[i] = dot(k_t, dss[j])
            attended.put(i, spread_heads(o16))
        dv = dot_nt(jnp.concatenate(g_t, axis=1), jnp.concatenate(p16s, axis=1))
        dk = dot_nt(jnp.concatenate(q_t, axis=1), jnp.concatenate(dss, axis=1))
        if first:
            acc_v[:, lo * BLK :] += dv
            acc_k[:, lo * BLK :] += dk
        else:
            acc_v[:, lo * BLK :] = dv
            acc_k[:, lo * BLK :] = dk

    def rectangle(lo, most):
        pair(lo, 0, most)
        for first in range(2, most, 2):

            @pl.when(here > first)
            def _(first=first):
                pair(lo, first, most)

        for i in range(most):

            @pl.when(here > i // 2 * 2)
            def _(i=i):
                attended.copy(i).wait()

        for c, acc, scale in ((0, acc_k, SCALE), (1, acc_v, 1.0)):
            whole = (acc[:, lo * BLK :] * scale).astype(BF16).T
            cols = slice(c * HD, (c + 1) * HD)
            if lo < far:
                d2_ref[lo * BLK :, cols] = whole[: (far - lo) * BLK]
            d1_ref[:, cols] = whole[(far - lo) * BLK :]

    @pl.when((here > 0) & (start >= far))
    def _():
        rectangle(far, blocks_dev)

    if far >= 1:

        @pl.when((here > 0) & (start == far - 1))
        def _():
            rectangle(far - 1, min(blocks_dev, MOST_BLK - blocks_dev - 1))

    if far >= 2:

        @pl.when((here > 0) & (start < far - 1))
        def _():
            rectangle(0, min(blocks_dev, MOST_BLK - blocks_dev - 2))


def own_backward(blocks_dev, heads, docs_ref, k_ref, v_ref, *rest):
    given, (query_ref, *outs), scratch = rest[: 4 * heads], rest[4 * heads : 6 * heads + 1], rest[6 * heads + 1 :]
    acc_k, acc_v, out_ref, sem = scratch
    base = lax.axis_index("ctx") * blocks_dev
    _, here = crossing(docs_ref, base, blocks_dev)
    for h in range(heads):
        qt_ref, gt_ref, ls_ref, dq_ref = given[4 * h : 4 * h + 4]
        store = Store(out_ref.at[h], sem.at[h], query_ref, h)
        k, v = k_ref[:, h * HD : (h + 1) * HD], v_ref[:, h * HD : (h + 1) * HD]
        k_t = k.T
        acc_k[h] = jnp.zeros_like(acc_k[h])
        acc_v[h] = jnp.zeros_like(acc_v[h])
        for i in range(blocks_dev):
            n = (i + 1) * BLK
            q_t, g_t = qt_ref[i], gt_ref[i]
            s = own_scores(k, q_t, i, blocks_behind(docs_ref, base + i))
            p = jnp.exp2(s - ls_ref[i : i + 1, :])
            acc_v[h, :, :n] += dot_nt(g_t, p.astype(BF16))
            ds = (p * (dot(v[:n], g_t) - ls_ref[blocks_dev + i : blocks_dev + i + 1, :])).astype(BF16)
            acc_k[h, :, :n] += dot_nt(q_t, ds)
            dq = dot(k_t[:, :n], ds) + jnp.where(i < here, dq_ref[i], 0.0)
            store.put(i, spread_heads((dq * SCALE).astype(BF16)))
        outs[2 * h][...] = (acc_k[h] * SCALE).T
        outs[2 * h + 1][...] = acc_v[h].T
    for h in range(heads):
        for i in range(blocks_dev):
            Store(out_ref.at[h], sem.at[h], query_ref, h).copy(i).wait()


def finish(heads, *refs):
    dk_out, dv_out = refs[4 * heads :]
    for h in range(heads):
        dk_ref, dv_ref, near_ref, far_ref = refs[4 * h : 4 * h + 4]
        skip = dk_ref.shape[0] - far_ref.shape[0]
        for out, own_ref, cols in ((dk_out, dk_ref, slice(0, HD)), (dv_out, dv_ref, slice(HD, 2 * HD))):
            whole = own_ref[...] + near_ref[:, cols].astype(F32)
            out[:skip, h * HD : (h + 1) * HD] = whole[:skip].astype(BF16)
            whole = whole[skip:] + far_ref[:, cols].astype(F32)
            out[skip:, h * HD : (h + 1) * HD] = whole.astype(BF16)


def body(queries, key_vecs, value_vecs, out_grad, doc_ids):
    length_dev = queries.shape[0]
    blocks_dev = length_dev // BLK
    heads = key_vecs.shape[1] // HD
    lanes = GROUP * BLK
    far = (MOST_BLK - 1 - blocks_dev) * BLK
    tile = (blocks_dev, HD, lanes)
    part = (length_dev, HD)
    out_blocks = [pltpu.VMEM((blocks_dev, BLK, WIDE), BF16), pltpu.SemaphoreType.DMA((blocks_dev,))]

    def call(kernel, args, outs, scratch=(), hbm_args=(), hbm_outs=(), alias=None):
        vmem = pl.BlockSpec(memory_space=pltpu.VMEM)
        smem = pl.BlockSpec(memory_space=pltpu.SMEM)
        hbm = pl.BlockSpec(memory_space=pltpu.HBM)
        return pl.pallas_call(
            kernel,
            in_specs=[hbm if i in hbm_args else smem if x.dtype == jnp.int32 else vmem for i, x in enumerate(args)],
            out_specs=[hbm if i in hbm_outs else vmem for i in range(len(outs))],
            out_shape=[jax.ShapeDtypeStruct(*out) for out in outs],
            scratch_shapes=scratch,
            input_output_aliases=alias or {},
            compiler_params=pltpu.CompilerParams(vmem_limit_bytes=24 << 20),
        )(*args)

    k1 = turn(key_vecs, 1)
    v1 = turn(value_vecs, 1)
    inputs = [pltpu.with_memory_space_constraint(x, pltpu.HBM) for x in (doc_ids, queries, out_grad, key_vecs, value_vecs)]
    per_head = [(tile, BF16), (tile, BF16), ((4 * blocks_dev, lanes), F32), (tile, F32)]
    attended, doc_ids, queries, out_grad, key_vecs, value_vecs, *outs = call(
        functools.partial(own_first, blocks_dev, heads),
        inputs,
        [(queries.shape, BF16), *((x.shape, x.dtype) for x in inputs), *per_head],
        [*out_blocks, pltpu.SMEM(doc_ids.shape, jnp.int32), pltpu.SemaphoreType.DMA((5, max(heads, 2)))],
        hbm_args=range(5),
        hbm_outs=(0,),
    )
    k1, outs[0] = lax.optimization_barrier((k1, outs[0]))
    k2 = turn(k1[length_dev - far :], 1)
    v2 = turn(v1[length_dev - far :], 1)
    first = [outs]
    for h in range(1, heads):
        args = [doc_ids, queries, out_grad, key_vecs, value_vecs, attended]
        attended, *outs = call(
            functools.partial(own_later, blocks_dev, h),
            args,
            [(queries.shape, BF16), *per_head],
            out_blocks,
            hbm_args=(5,),
            hbm_outs=(0,),
            alias={5: 0},
        )
        first.append(outs)

    given, returned = [], []
    for h in range(heads):
        q_t, g_t, stats, o0 = first[h]
        args = [doc_ids, q_t, g_t, k1, v1, k2, v2, stats, o0, attended]
        attended, dq, ls, d1, d2 = call(
            functools.partial(far_part, blocks_dev, h),
            args,
            [
                (queries.shape, BF16),
                (tile, F32),
                ((2 * blocks_dev, lanes), F32),
                ((length_dev, 2 * HD), BF16),
                ((far, 2 * HD), BF16),
            ],
            [pltpu.VMEM((HD, length_dev + far), F32)] * 2 + out_blocks,
            hbm_args=(len(args) - 1,),
            hbm_outs=(0,),
            alias={len(args) - 1: 0},
        )
        given += [q_t, g_t, ls, dq]
        d1 = turn(d1, -1)
        d2 = turn(d2, -2)
        returned.append((d1, d2))

    query_grad, *own = call(
        functools.partial(own_backward, blocks_dev, heads),
        [doc_ids, key_vecs, value_vecs, *given],
        [(queries.shape, BF16)] + [(part, F32)] * (2 * heads),
        [pltpu.VMEM((heads, HD, length_dev), F32)] * 2
        + [pltpu.VMEM((heads, blocks_dev, BLK, WIDE), BF16), pltpu.SemaphoreType.DMA((heads, blocks_dev))],
        hbm_outs=(0,),
    )
    args = [x for h in range(heads) for x in (*own[2 * h : 2 * h + 2], *returned[h])]
    key_grad, value_grad = call(functools.partial(finish, heads), args, [(key_vecs.shape, BF16)] * 2)
    return (attended, query_grad, key_grad, value_grad)


def solution(mesh):
    placed = (P("ctx", "tp"), P("ctx", "tp"), P("ctx", "tp"), P("ctx", "tp"), P())
    return jax.shard_map(
        body,
        mesh=mesh,
        in_specs=placed,
        out_specs=(P("ctx", "tp"), P("ctx", "tp"), P("ctx", "tp"), P("ctx", "tp")),
        check_vma=False,
    )
```

```python
import functools

import jax
import jax.numpy as jnp
from jax import lax
from jax.experimental import pallas as pl
from jax.experimental.pallas import tpu as pltpu
from jax.sharding import PartitionSpec as P

QH = 32
KVH = 8
HD = 128
BLK = 128
MOST_BLK = 8
GROUP = QH // KVH
SCALE = HD ** (-0.5)
WIDE = GROUP * HD
LOG2E = 1.4426950408889634
SCALE2 = SCALE * LOG2E
negative_fill = -1e30
F32 = jnp.float32
BF16 = jnp.bfloat16


def turn(block, step, around=True):
    n = lax.axis_size("ctx")
    return lax.ppermute(block, "ctx", [(i, (i + step) % n) for i in range(n) if around or 0 <= i + step < n])


def dot(a, b):
    return lax.dot_general(a, b, (((1,), (0,)), ((), ())), preferred_element_type=F32)


def dot_nt(a, b):
    return lax.dot_general(a, b, (((1,), (1,)), ((), ())), preferred_element_type=F32)


def stack_heads(x):
    return jnp.concatenate([x[:, g * HD : (g + 1) * HD] for g in range(GROUP)], axis=0).T


def spread_heads(x):
    x = x.T
    rows = x.shape[0] // GROUP
    return jnp.concatenate([x[g * rows : (g + 1) * rows] for g in range(GROUP)], axis=1)


def blocks_behind(docs_ref, index):
    doc = docs_ref[index]
    count = jnp.int32(0)
    for d in range(1, MOST_BLK):
        same = (index >= d) & (docs_ref[jnp.maximum(index - d, 0)] == doc)
        count = count + jnp.where(same, 1, 0)
    return count


def crossing(docs_ref, base, blocks_dev):
    behind = blocks_behind(docs_ref, base)
    here = jnp.int32(0)
    for i in range(blocks_dev):
        here = here + jnp.where(docs_ref[base + i] == docs_ref[base], 1, 0)
    return behind, jnp.where(behind > 0, here, 0)


def biased(s, first, start):
    parts = []
    for b in range(s.shape[0] // BLK):
        bias = jnp.where(first + b >= start, 0.0, negative_fill).astype(F32)
        parts.append(s[b * BLK : (b + 1) * BLK] * SCALE2 + bias)
    return parts


def causal(part):
    key = lax.broadcasted_iota(jnp.int32, part.shape, 0)
    query = lax.broadcasted_iota(jnp.int32, part.shape, 1) % BLK
    return jnp.where(key <= query, part, negative_fill)


def own_scores(k, q_t, i, behind):
    parts = biased(dot(k[: (i + 1) * BLK], q_t), 0, i - behind)
    parts[i] = causal(parts[i])
    return jnp.concatenate(parts, axis=0)


def delta_of(o16, g_t):
    return jnp.sum(o16.astype(F32) * g_t.astype(F32), axis=0, keepdims=True)


class Store:
    def __init__(self, blocks, sem, whole, head):
        self.blocks, self.sem, self.whole, self.head = blocks, sem, whole, head

    def copy(self, i):
        place = self.whole.at[pl.ds(i * BLK, BLK), pl.ds(self.head * WIDE, WIDE)]
        return pltpu.make_async_copy(self.blocks.at[i], place, self.sem.at[i])

    def put(self, i, x):
        self.blocks[i] = x
        self.copy(i).start()


def own_part(blocks_dev, head, docs_ref, q_ref, g_ref, k_ref, v_ref, att_ref, qt_ref, gt_ref, stats_ref, o_ref, out_ref, sem):
    attended = Store(out_ref, sem, att_ref, head)
    base = lax.axis_index("ctx") * blocks_dev
    wide, slim = slice(head * WIDE, (head + 1) * WIDE), slice(head * HD, (head + 1) * HD)
    k = k_ref[:, slim]
    v_t = v_ref[:, slim].T
    for i in range(blocks_dev):
        rows = slice(i * BLK, (i + 1) * BLK)
        q_t = stack_heads(q_ref[rows, wide])
        g_t = stack_heads(g_ref[rows, wide])
        qt_ref[i] = q_t
        gt_ref[i] = g_t
        s = own_scores(k, q_t, i, blocks_behind(docs_ref, base + i))
        m = jnp.max(s, axis=0, keepdims=True)
        p = jnp.exp2(s - m)
        l = jnp.sum(p, axis=0, keepdims=True)
        o = dot(v_t[:, : (i + 1) * BLK], p.astype(BF16))
        o_ref[i] = o
        o16 = (o * (1.0 / l)).astype(BF16)
        attended.put(i, spread_heads(o16))
        for r, row in enumerate((m, l, m + jnp.log2(l), delta_of(o16, g_t))):
            stats_ref[r * blocks_dev + i : r * blocks_dev + i + 1, :] = row
    for i in range(blocks_dev):
        attended.copy(i).wait()


def own_first(blocks_dev, heads, *refs):
    sources, att_ref, targets, outs = refs[:5], refs[5], refs[6:11], refs[11:15]
    out_ref, sem, docs_smem, read_sem = refs[15:]
    docs = pltpu.make_async_copy(sources[0], docs_smem, read_sem.at[0, 0])
    docs_out = pltpu.make_async_copy(sources[0], targets[0], read_sem.at[0, 1])
    reads = []
    for a in range(1, 5):
        width = sources[a].shape[1] // heads
        for h in range(heads):
            part = (slice(None), pl.ds(h * width, width))
            reads.append((h, pltpu.make_async_copy(sources[a].at[part], targets[a].at[part], read_sem.at[a, h])))
    reads.sort(key=lambda read: read[0])
    docs.start()
    for _, read in reads:
        read.start()
    docs_out.start()
    docs.wait()
    for h, read in reads:
        if h == 0:
            read.wait()
    own_part(blocks_dev, 0, docs_smem, *targets[1:], att_ref, *outs, out_ref, sem)
    for h, read in reads:
        if h > 0:
            read.wait()
    docs_out.wait()


def own_later(blocks_dev, head, docs_ref, q_ref, g_ref, k_ref, v_ref, _, *rest):
    own_part(blocks_dev, head, docs_ref, q_ref, g_ref, k_ref, v_ref, *rest)


def over_variants(docs_ref, blocks_dev, far, run):
    behind, here = crossing(docs_ref, lax.axis_index("ctx") * blocks_dev, blocks_dev)
    start = blocks_dev + far - behind
    cases = [(far, blocks_dev, start >= far)]
    if far >= 1:
        cases.append((far - 1, min(blocks_dev, MOST_BLK - blocks_dev - 1), start == far - 1))
    if far >= 2:
        cases.append((0, min(blocks_dev, MOST_BLK - blocks_dev - 2), start < far - 1))
    for lo, most, case in cases:

        @pl.when((here > 0) & case)
        def _(lo=lo, most=most):
            run(lo, most, start, here)


def window(near_ref, far_ref, cols, lo):
    piece = near_ref[:, cols]
    if lo * BLK < far_ref.shape[0]:
        piece = jnp.concatenate([far_ref[lo * BLK :, cols], piece], axis=0)
    return piece


def in_pairs(most, here, run):
    run(range(0, min(2, most)))
    for first in range(2, most, 2):

        @pl.when(here > first)
        def _(first=first):
            run(range(first, min(first + 2, most)))


def give_back(acc, lo, far, scale, cols, near_ref, far_ref):
    whole = (acc[:, lo * BLK :] * scale).astype(BF16).T
    if lo < far:
        far_ref[lo * BLK :, cols] = whole[: (far - lo) * BLK]
    near_ref[:, cols] = whole[(far - lo) * BLK :]


def accumulate(acc, lo, fresh, x):
    if fresh:
        acc[:, lo * BLK :] = x
    else:
        acc[:, lo * BLK :] += x


def far_keys(blocks_dev, heads, docs_ref, k1_ref, k2_ref, *rest):
    given, (near_ref, far_ref, *outs), acc = rest[: 3 * heads], rest[3 * heads : -1], rest[-1]
    far = k2_ref.shape[0] // BLK
    reach = blocks_dev + far
    near_ref[...] = jnp.zeros_like(near_ref)
    far_ref[...] = jnp.zeros_like(far_ref)

    def run(lo, most, start, here):
        for h in range(heads):
            qt_ref, gt_ref, stats_ref = given[3 * h : 3 * h + 3]
            p_ref, rows_ref = outs[2 * h : 2 * h + 2]
            cols = slice(h * HD, (h + 1) * HD)

            def pair(blocks, qt_ref=qt_ref, gt_ref=gt_ref, stats_ref=stats_ref, p_ref=p_ref, rows_ref=rows_ref, cols=cols):
                k = window(k1_ref, k2_ref, cols, lo)
                scores = [dot(k, qt_ref[i]) for i in blocks]
                weights = []
                for s, i in zip(scores, blocks):
                    m0 = stats_ref[i : i + 1, :]
                    s = jnp.concatenate(biased(s, lo, jnp.where(i < here, start, reach)), axis=0)
                    m = jnp.maximum(m0, jnp.max(s, axis=0, keepdims=True))
                    p = jnp.exp2(s - m)
                    shrink = jnp.exp2(m0 - m)
                    l = stats_ref[blocks_dev + i : blocks_dev + i + 1, :] * shrink + jnp.sum(p, axis=0, keepdims=True)
                    inv = 1.0 / l
                    p16 = (p * inv).astype(BF16)
                    p_ref[i, lo * BLK :, :] = p16
                    weights.append(p16)
                    rows_ref[i : i + 1, :] = m + jnp.log2(l)
                    rows_ref[blocks_dev + i : blocks_dev + i + 1, :] = shrink * inv
                g_t = jnp.concatenate([gt_ref[i] for i in blocks], axis=1)
                accumulate(acc, lo, blocks[0] == 0, dot_nt(g_t, jnp.concatenate(weights, axis=1)))

            in_pairs(most, here, pair)
            give_back(acc, lo, far, 1.0, cols, near_ref, far_ref)

    over_variants(docs_ref, blocks_dev, far, run)


def far_values(blocks_dev, heads, docs_ref, k1_ref, k2_ref, v1_ref, v2_ref, *rest):
    given, rest = rest[: 6 * heads], rest[6 * heads + 1 :]
    (att_ref, near_ref, far_ref, *outs), (acc, out_ref, sem) = rest[:-3], rest[-3:]
    far = k2_ref.shape[0] // BLK
    near_ref[...] = jnp.zeros_like(near_ref)
    far_ref[...] = jnp.zeros_like(far_ref)
    for h in range(heads):
        outs[2 * h + 1][...] = given[6 * h + 2][2 * blocks_dev :, :]

    def run(lo, most, start, here):
        for h in range(heads):
            cols = slice(h * HD, (h + 1) * HD)
            attended = Store(out_ref.at[h], sem.at[h], att_ref, h)

            def pair(blocks, h=h, cols=cols, attended=attended):
                qt_ref, gt_ref, _, o0_ref, p_ref, rows_ref = given[6 * h : 6 * h + 6]
                dq_ref, ls_ref = outs[2 * h : 2 * h + 2]
                k, v = window(k1_ref, k2_ref, cols, lo), window(v1_ref, v2_ref, cols, lo)
                k_t, v_t = k.T, v.T
                ps = [p_ref[i, lo * BLK :, :] for i in blocks]
                grads = [gt_ref[i] for i in blocks]
                keep = [rows_ref[blocks_dev + i : blocks_dev + i + 1, :] for i in blocks]
                attended16 = [
                    (dot(v_t, p) + o0_ref[i] * scale).astype(BF16) for p, i, scale in zip(ps, blocks, keep)
                ]
                dps = [dot(v, g) for g in grads]
                dss = []
                for p, dp, o16, g, i in zip(ps, dps, attended16, grads, blocks):
                    delta = delta_of(o16, g)
                    ls_ref[i : i + 1, :] = rows_ref[i : i + 1, :]
                    ls_ref[blocks_dev + i : blocks_dev + i + 1, :] = delta
                    ds = (p.astype(F32) * (dp - delta)).astype(BF16)
                    dq_ref[i] = dot(k_t, ds)
                    dss.append(ds)
                    attended.put(i, spread_heads(o16))
                q_t = jnp.concatenate([qt_ref[i] for i in blocks], axis=1)
                accumulate(acc, lo, blocks[0] == 0, dot_nt(q_t, jnp.concatenate(dss, axis=1)))

            in_pairs(most, here, pair)
            give_back(acc, lo, far, SCALE, cols, near_ref, far_ref)
        for h in range(heads):
            for i in range(most):

                @pl.when(here > i // 2 * 2)
                def _(h=h, i=i):
                    Store(out_ref.at[h], sem.at[h], att_ref, h).copy(i).wait()

    over_variants(docs_ref, blocks_dev, far, run)


def own_backward(blocks_dev, heads, docs_ref, k_ref, v_ref, *rest):
    given, (query_ref, *outs), scratch = rest[: 4 * heads], rest[4 * heads : 6 * heads + 1], rest[6 * heads + 1 :]
    acc_k, acc_v, out_ref, sem = scratch
    base = lax.axis_index("ctx") * blocks_dev
    _, here = crossing(docs_ref, base, blocks_dev)
    for h in range(heads):
        qt_ref, gt_ref, ls_ref, dq_ref = given[4 * h : 4 * h + 4]
        store = Store(out_ref.at[h], sem.at[h], query_ref, h)
        k, v = k_ref[:, h * HD : (h + 1) * HD], v_ref[:, h * HD : (h + 1) * HD]
        k_t = k.T
        acc_k[h] = jnp.zeros_like(acc_k[h])
        acc_v[h] = jnp.zeros_like(acc_v[h])
        for i in range(blocks_dev):
            n = (i + 1) * BLK
            q_t, g_t = qt_ref[i], gt_ref[i]
            s = own_scores(k, q_t, i, blocks_behind(docs_ref, base + i))
            p = jnp.exp2(s - ls_ref[i : i + 1, :])
            acc_v[h, :, :n] += dot_nt(g_t, p.astype(BF16))
            ds = (p * (dot(v[:n], g_t) - ls_ref[blocks_dev + i : blocks_dev + i + 1, :])).astype(BF16)
            acc_k[h, :, :n] += dot_nt(q_t, ds)
            dq = dot(k_t[:, :n], ds) + jnp.where(i < here, dq_ref[i], 0.0)
            store.put(i, spread_heads((dq * SCALE).astype(BF16)))
        outs[2 * h][...] = (acc_k[h] * SCALE).T
        outs[2 * h + 1][...] = acc_v[h].T
    for h in range(heads):
        for i in range(blocks_dev):
            Store(out_ref.at[h], sem.at[h], query_ref, h).copy(i).wait()


def finish(heads, *refs):
    returned, (dk_out, dv_out) = refs[2 * heads : 2 * heads + 4], refs[2 * heads + 4 :]
    for h in range(heads):
        cols = slice(h * HD, (h + 1) * HD)
        for c, out in enumerate((dk_out, dv_out)):
            own_ref, near_ref, far_ref = refs[2 * h + c], returned[2 * c], returned[2 * c + 1]
            skip = own_ref.shape[0] - far_ref.shape[0]
            whole = own_ref[...] + near_ref[:, cols].astype(F32)
            out[:skip, cols] = whole[:skip].astype(BF16)
            out[skip:, cols] = (whole[skip:] + far_ref[:, cols].astype(F32)).astype(BF16)


def body(queries, key_vecs, value_vecs, out_grad, doc_ids):
    length_dev = queries.shape[0]
    blocks_dev = length_dev // BLK
    heads = key_vecs.shape[1] // HD
    lanes = GROUP * BLK
    far = (MOST_BLK - 1 - blocks_dev) * BLK
    tile = (blocks_dev, HD, lanes)
    part = (length_dev, HD)
    key_grad_shape = key_vecs.shape
    out_blocks = [pltpu.VMEM((blocks_dev, BLK, WIDE), BF16), pltpu.SemaphoreType.DMA((blocks_dev,))]

    def call(kernel, args, outs, scratch=(), hbm_args=(), hbm_outs=(), alias=None):
        vmem = pl.BlockSpec(memory_space=pltpu.VMEM)
        smem = pl.BlockSpec(memory_space=pltpu.SMEM)
        hbm = pl.BlockSpec(memory_space=pltpu.HBM)
        return pl.pallas_call(
            kernel,
            in_specs=[hbm if i in hbm_args else smem if x.dtype == jnp.int32 else vmem for i, x in enumerate(args)],
            out_specs=[hbm if i in hbm_outs else vmem for i in range(len(outs))],
            out_shape=[jax.ShapeDtypeStruct(*out) for out in outs],
            scratch_shapes=scratch,
            input_output_aliases=alias or {},
            compiler_params=pltpu.CompilerParams(vmem_limit_bytes=24 << 20),
        )(*args)

    k1 = turn(key_vecs, 1)
    v1 = turn(value_vecs, 1)
    inputs = [pltpu.with_memory_space_constraint(x, pltpu.HBM) for x in (doc_ids, queries, out_grad, key_vecs, value_vecs)]
    per_head = [(tile, BF16), (tile, BF16), ((4 * blocks_dev, lanes), F32), (tile, F32)]
    attended, doc_ids, queries, out_grad, key_vecs, value_vecs, *outs = call(
        functools.partial(own_first, blocks_dev, heads),
        inputs,
        [(queries.shape, BF16), *((x.shape, x.dtype) for x in inputs), *per_head],
        [*out_blocks, pltpu.SMEM(doc_ids.shape, jnp.int32), pltpu.SemaphoreType.DMA((5, max(heads, 2)))],
        hbm_args=range(5),
        hbm_outs=(0,),
    )
    k1, outs[0] = lax.optimization_barrier((k1, outs[0]))
    k2 = turn(k1[length_dev - far :], 1)
    first = [outs]
    for h in range(1, heads):
        args = [doc_ids, queries, out_grad, key_vecs, value_vecs, attended]
        attended, *outs = call(
            functools.partial(own_later, blocks_dev, h),
            args,
            [(queries.shape, BF16), *per_head],
            out_blocks,
            hbm_args=(5,),
            hbm_outs=(0,),
            alias={5: 0},
        )
        first.append(outs)
    v1, first[-1][0] = lax.optimization_barrier((v1, first[-1][0]))
    v2 = turn(v1[length_dev - far :], 1)

    both = [((length_dev, heads * HD), BF16), ((far, heads * HD), BF16)]
    acc = pltpu.VMEM((HD, length_dev + far), F32)
    args = [doc_ids, k1, k2] + [x for q_t, g_t, stats, _ in first for x in (q_t, g_t, stats)]
    near_v, far_v, *weights = call(
        functools.partial(far_keys, blocks_dev, heads),
        args,
        both + [((blocks_dev, length_dev + far, lanes), BF16), ((2 * blocks_dev, lanes), F32)] * heads,
        [acc],
    )
    near_v = turn(near_v, -1)
    far_v = turn(far_v, -2, False)

    args = [doc_ids, k1, k2, v1, v2] + [x for h in range(heads) for x in (*first[h], *weights[2 * h : 2 * h + 2])]
    args.append(attended)
    attended, near_k, far_k, *outs = call(
        functools.partial(far_values, blocks_dev, heads),
        args,
        [(queries.shape, BF16), *both] + [(tile, F32), ((2 * blocks_dev, lanes), F32)] * heads,
        [
            acc,
            pltpu.VMEM((heads, blocks_dev, BLK, WIDE), BF16),
            pltpu.SemaphoreType.DMA((heads, blocks_dev)),
        ],
        hbm_args=(len(args) - 1,),
        hbm_outs=(0,),
        alias={len(args) - 1: 0},
    )
    near_k = turn(near_k, -1)
    far_k = turn(far_k, -2)

    given = [x for h in range(heads) for x in (*first[h][:2], outs[2 * h + 1], outs[2 * h])]
    query_grad, *own = call(
        functools.partial(own_backward, blocks_dev, heads),
        [doc_ids, key_vecs, value_vecs, *given],
        [(queries.shape, BF16)] + [(part, F32)] * (2 * heads),
        [pltpu.VMEM((heads, HD, length_dev), F32)] * 2
        + [pltpu.VMEM((heads, blocks_dev, BLK, WIDE), BF16), pltpu.SemaphoreType.DMA((heads, blocks_dev))],
        hbm_outs=(0,),
    )
    key_grad, value_grad = call(
        functools.partial(finish, heads), [*own, near_k, far_k, near_v, far_v], [(key_grad_shape, BF16)] * 2
    )
    return (attended, query_grad, key_grad, value_grad)


def solution(mesh):
    placed = (P("ctx", "tp"), P("ctx", "tp"), P("ctx", "tp"), P("ctx", "tp"), P())
    return jax.shard_map(
        body,
        mesh=mesh,
        in_specs=placed,
        out_specs=(P("ctx", "tp"), P("ctx", "tp"), P("ctx", "tp"), P("ctx", "tp")),
        check_vma=False,
    )
```
